128 devices in a mesh: fsdp: 16 (over y, x), group: 8 (over z, core).
Axes of the slice: x: 4, y: 4, z: 4, core: 2. Of those that a mesh axis runs over, the one named last changes fastest.
Arguments:
- gradients: bfloat16 [128, 512, 512], P('group', 'fsdp'), may hold values from -6 to 6
- owners: int32 [8, 16], P('group'), may hold values from 0 to 15, each once within a row
- left_factors: float32 [128, 512, 512], P(('fsdp', 'group')), may hold values from -60 to 800, as said below
- right_factors: float32 [128, 512, 512], P(('fsdp', 'group')), may hold values from -60 to 800, as said below
- left_bases: float32 [128, 512, 512], P(('fsdp', 'group')), may hold values from -1 to 1
- right_bases: float32 [128, 512, 512], P(('fsdp', 'group')), may hold values from -1 to 1
- moments: float32 [128, 512, 512], P(('fsdp', 'group')), may hold values from 0.04 to 600
Outputs:
- updates: bfloat16 [128, 512, 512], P('group', 'fsdp')
The draws below stay inside these ranges and needn't reach their ends.
Inputs may be any that keep to these rules, and one draw needn't show every extreme that they name: Each row of owners is a permutation of the 16 indices along fsdp. `left_factors`: each block is symmetric and positive definite. `right_factors`: each block is symmetric and positive definite.
All inputs are finite; a program needn't handle non-finite values.
Results may differ from the reference program's by a relative error of at most 0.01.
Values may be sent and summed in bfloat16 or wider, within the bound.
No kernel may reach another device: no remote copies, remote signals or barrier semaphores. Data moves between devices by JAX's collectives and lax.ppermute only.
A program may use at most 64 MiB of HBM per device.

```python
import jax
import jax.numpy as jnp
from jax import lax

B = 512
BLOCKS = 128
N_FSDP = 16
N_GROUP = 8


def definite(key):
    first_key, second_key = jax.random.split(key)
    level, bottom, top = (40.0, 0.5, 5.0)
    diagonal = jnp.exp(jax.random.uniform(first_key, (BLOCKS, B), jnp.float32, jnp.log(bottom), jnp.log(top)))
    random_rows = jax.random.normal(second_key, (BLOCKS, B, B), jnp.float32)

    def square(matrix):
        return jnp.dot(matrix, matrix.T, precision=lax.Precision.HIGHEST) / B
    crossed = lax.map(square, random_rows)
    return level * (crossed + diagonal[:, :, None] * jnp.eye(B, dtype=jnp.float32))


def orthonormal(key):
    random_rows = jax.random.normal(key, (BLOCKS, B, B), jnp.float32)
    basis_out, _ = jnp.linalg.qr(random_rows)
    return basis_out.astype(jnp.float32)


def draw_left_factors(key, part):
    return definite(jax.random.fold_in(key, 11))


def draw_right_factors(key, part):
    return definite(jax.random.fold_in(key, 12))


def draw_left_bases(key, part):
    return orthonormal(jax.random.fold_in(key, 13))


def draw_right_bases(key, part):
    return orthonormal(jax.random.fold_in(key, 14))


def draw_moments(key, part):
    row_key, column_key, entry_key = jax.random.split(jax.random.fold_in(key, 15), 3)
    level, spread = (0.1, 10.0)
    row_scale = jnp.exp(jax.random.uniform(row_key, (BLOCKS, B, 1), jnp.float32, 0.0, jnp.log(spread)))
    column_scale = jnp.exp(jax.random.uniform(column_key, (BLOCKS, 1, B), jnp.float32, 0.0, jnp.log(spread)))
    entries = jax.random.uniform(entry_key, (BLOCKS, B, B), jnp.float32, 0.5, 2.0)
    positions = jnp.arange(BLOCKS, dtype=jnp.float32)
    falling = 3.0 / (1.0 + 2.0 * positions / max(BLOCKS - 1, 1))
    return level * falling[:, None, None] * row_scale * column_scale * entries


def levels(stream_key, shape, shards, low, top_value):
    def one(axis_at, blocks):
        steps = jax.random.uniform(jax.random.fold_in(jax.random.fold_in(stream_key, 6), axis_at), (blocks,), jnp.float32, low / len(shards), top_value / len(shards))
        return jnp.repeat(jnp.exp(steps), shape[axis_at] // blocks).reshape((-1,) + (1,) * (len(shape) - axis_at - 1))

    loudness = one(*shards[0])
    for cut in shards[1:]:
        loudness = loudness * one(*cut)
    return loudness


def centred(stream_key, dims, deviation, most, cuts=(), kind=jnp.bfloat16):
    values = deviation * jax.random.normal(stream_key, dims, jnp.float32)
    if cuts:
        values = values * levels(stream_key, dims, cuts, -0.22, 0.18)
    return jnp.clip(values, -most, most).astype(kind)


def setup_inputs(seed: int = 0) -> dict:
    splits = jax.random.split(jax.random.key(seed), 8)
    gradients = centred(splits[0], (BLOCKS, B, B), 1.0, 6.0, ((0, 8), (1, 16)))
    owners = jax.vmap(lambda own: jax.random.permutation(own, N_FSDP))(jax.random.split(splits[1], N_GROUP)).reshape((N_GROUP, N_FSDP)).astype(jnp.int32)
    left_factors = draw_left_factors(jax.random.fold_in(splits[7], 71), 0)
    right_factors = draw_right_factors(jax.random.fold_in(splits[7], 71), 0)
    left_bases = draw_left_bases(jax.random.fold_in(splits[7], 71), 0)
    right_bases = draw_right_bases(jax.random.fold_in(splits[7], 71), 0)
    moments = draw_moments(jax.random.fold_in(splits[7], 71), 0)
    return dict(gradients=gradients, owners=owners, left_factors=left_factors, right_factors=right_factors, left_bases=left_bases, right_bases=right_bases, moments=moments)


factor_decay = 0.95
moment_decay = 0.95
epsilon = 1e-08
clip_rms = 0.25

def refresh(factor, old_basis):
    projected = jnp.dot(factor, old_basis, precision=lax.Precision.HIGHEST)
    correlation = jnp.dot(projected.T, projected, precision=lax.Precision.HIGHEST)
    cholesky_factor = jnp.linalg.cholesky(correlation)
    solved = jax.scipy.linalg.solve_triangular(cholesky_factor, projected.T, lower=True)
    return solved.T.astype(jnp.bfloat16)

def precondition(gradient, left_old, right_old, left_basis, right_basis, moment):
    left_gram = jnp.dot(gradient.astype(jnp.float32), gradient.T.astype(jnp.float32), preferred_element_type=jnp.float32)
    right_gram = jnp.dot(gradient.T.astype(jnp.float32), gradient.astype(jnp.float32), preferred_element_type=jnp.float32)
    left_new = factor_decay * left_old + (1.0 - factor_decay) * left_gram
    right_new = factor_decay * right_old + (1.0 - factor_decay) * right_gram
    left_rotate = refresh(left_new, left_basis)
    right_rotate = refresh(right_new, right_basis)
    first = jnp.dot(left_rotate.T.astype(jnp.float32), gradient.astype(jnp.float32), preferred_element_type=jnp.float32).astype(jnp.bfloat16)
    rotated = jnp.dot(first.astype(jnp.float32), right_rotate.astype(jnp.float32), preferred_element_type=jnp.float32)
    moment_new = moment_decay * moment + (1.0 - moment_decay) * rotated * rotated
    normed = (rotated / (jnp.sqrt(moment_new) + epsilon)).astype(jnp.bfloat16)
    back = jnp.dot(left_rotate.astype(jnp.float32), normed.astype(jnp.float32), preferred_element_type=jnp.float32).astype(jnp.bfloat16)
    return jnp.dot(back.astype(jnp.float32), right_rotate.T.astype(jnp.float32), preferred_element_type=jnp.float32)

def reference(gradients, owners, left_factors, right_factors, left_bases, right_bases, moments):
    slot_table = owners.astype(jnp.int32) * N_GROUP + jnp.arange(N_GROUP, dtype=jnp.int32)[:, None]
    slot_list = slot_table.reshape(-1).astype(jnp.int32)

    def single(pair):
        gradient, slot = pair

        def pick(states):
            return lax.dynamic_index_in_dim(states, slot, 0, keepdims=False)
        return precondition(gradient, pick(left_factors), pick(right_factors), pick(left_bases), pick(right_bases), pick(moments))
    unclipped = lax.map(single, (gradients, slot_list))
    total = jnp.sum(unclipped * unclipped)
    count = jnp.asarray(BLOCKS * B * B, jnp.float32)
    scale = jnp.minimum(1.0, clip_rms * jnp.sqrt(count) / jnp.sqrt(total + 1e-06))
    return (scale * unclipped).astype(jnp.bfloat16)
```

```python
import jax
import jax.numpy as jnp
from jax import lax
from jax.experimental import pallas as pl
from jax.experimental.pallas import tpu as pltpu
from jax.sharding import Mesh
from jax.sharding import PartitionSpec as P

SUB=8; NB=64
def sb(x, i):
    return jnp.broadcast_to(x[i:i + 1, :], x.shape)
def lanes(x, idx):
    return jnp.take_along_axis(x, idx, axis=1, mode="promise_in_bounds")
def recip(p):
    r = pl.reciprocal(p, approx=True)
    return r * (2.0 - p * r)
def invert_pair(D):
    count = NB // SUB
    sub = lax.broadcasted_iota(jnp.int32, (SUB, 128), 0)
    lane = lax.broadcasted_iota(jnp.int32, (SUB, 128), 1)
    half = lane // NB * NB
    col = lane - half
    here = [sub == i for i in range(SUB)]
    A = [D[SUB * r:SUB * (r + 1), :] for r in range(count)]
    W = [None] * count
    for s in range(count):
        base = SUB * s
        in_strip = (col >= base) & (col < base + SUB)
        unit = jnp.where(col == base + sub, 1.0, 0.0).astype(jnp.float32)
        idx = [half + (base + i) for i in range(SUB)]
        S = A[s]
        c = [lanes(S, idx[i]) for i in range(SUB)]
        S = jnp.where(in_strip, unit, S)
        for i in range(SUB):
            p = sb(c[i], i)
            rinv = recip(p)
            h = jnp.where(here[i], 1.0, -c[i])
            row = sb(S, i)
            U = row if i == 0 else jnp.where(here[i], S, U)
            rs = lax.rsqrt(p)
            scale = rs if i == 0 else jnp.where(here[i], rs, scale)
            S = jnp.where(here[i], 0.0, S) + h * (rinv * row)
            for n in range(i + 1, SUB):
                c[n] = jnp.where(here[i], 0.0, c[n]) + h * (rinv * sb(c[n], i))
        W[s] = jnp.where(col < base + SUB, U * scale, 0.0)
        z = [sb(S, i) for i in range(SUB)]
        for r in range(s + 1, count):
            X = A[r]
            acc = jnp.where(in_strip, 0.0, X)
            t0 = lanes(X, idx[0]) * z[0]
            t1 = lanes(X, idx[1]) * z[1]
            for i in range(2, SUB, 2):
                t0 = t0 + lanes(X, idx[i]) * z[i]
                t1 = t1 + lanes(X, idx[i + 1]) * z[i + 1]
            A[r] = acc - (t0 + t1)
    return jnp.concatenate(W, axis=0)


B = 512
HI = lax.Precision.HIGHEST
F32 = jnp.float32
BF = jnp.bfloat16


def dot(a, b, ca, cb, p=None):
    return lax.dot_general(a, b, (((ca,), (cb,)), ((), ())), precision=p, preferred_element_type=F32)


def nn(a, b, p=HI):
    return dot(a, b, 1, 0, p)


def nt(a, b, p=HI):
    return dot(a, b, 1, 1, p)


def tn(a, b, p=HI):
    return dot(a, b, 0, 0, p)


def left_half(shape):
    return lax.broadcasted_iota(jnp.int32, shape, 1) < 64


def spread(x):
    left = left_half(x.shape)
    return jnp.concatenate([jnp.where(left, x, 0.0), jnp.where(left, 0.0, x)], axis=0)


def invert_128(left, right):
    half = left_half((64, 128))
    turn = lambda x: pltpu.roll(x, 64, 1)
    first = jnp.where(half, left[:64], turn(right[:64]))
    below = jnp.where(half, left[64:], turn(right[64:]))
    last = jnp.where(half, turn(left[64:]), right[64:])
    w1 = invert_pair(first)
    w1d = spread(w1)
    k = nt(below, w1d)
    w2 = invert_pair(last - nt(k, spread(k)))
    w21 = -nn(w2, spread(nn(k, w1d)))
    zero = jnp.zeros((64, 128), F32)
    wl = jnp.concatenate([jnp.where(half, w1, zero), jnp.where(half, w21, turn(w2))], axis=0)
    wr = jnp.concatenate([jnp.where(half, turn(w1), zero), jnp.where(half, turn(w21), w2)], axis=0)
    return wl, wr


def kernel(g_ref, l0, r0, ql0, qr0, v0, out_ref, sum_ref, p_scr, c_scr, q_scr, n_scr):
    sides = (0, 1)
    g = g_ref[...]
    p_scr[0] = nn(0.95 * l0[...] + 0.05 * nt(g, g, None), ql0[...])
    p_scr[1] = nn(0.95 * r0[...] + 0.05 * tn(g, g, None), qr0[...])
    for m in sides:
        c_scr[m, :, 0:256] = tn(p_scr[m], p_scr[m, :, 0:256])
        c_scr[m, 256:, 256:] = tn(p_scr[m, :, 256:], p_scr[m, :, 256:])

    def half(o):
        a, b, e = o, o + 128, o + 256
        w1 = invert_128(c_scr[0, a:b, a:b], c_scr[1, a:b, a:b])
        k = [nt(c_scr[m, b:e, a:b], w1[m]) for m in sides]
        w2 = invert_128(*[c_scr[m, b:e, b:e] - nt(k[m], k[m]) for m in sides])
        return w1, k, w2

    w1, k, w2 = half(0)
    w = []
    for m in sides:
        w21 = -nn(w2[m], nn(k[m], w1[m]))
        w.append(jnp.concatenate([
            jnp.concatenate([w1[m], jnp.zeros((128, 128), F32)], axis=1),
            jnp.concatenate([w21, w2[m]], axis=1)], axis=0))
    for m in sides:
        k = nt(c_scr[m, 256:, 0:256], w[m])
        c_scr[m, 256:, 256:] = c_scr[m, 256:, 256:] - nt(k, k)
        q = nt(p_scr[m, :, 0:256], w[m])
        q_scr[m, :, 0:256] = q.astype(BF)
        p_scr[m, :, 256:] = p_scr[m, :, 256:] - nt(q, k)
    w1, k, w2 = half(256)
    for m in sides:
        q = nt(p_scr[m, :, 256:384], w1[m])
        q_scr[m, :, 256:384] = q.astype(BF)
        q = nt(p_scr[m, :, 384:512] - nt(q, k[m]), w2[m])
        q_scr[m, :, 384:512] = q.astype(BF)
    f = tn(q_scr[0], g, None).astype(BF)
    h = nn(f, q_scr[1], None)
    v = 0.95 * v0[...] + 0.05 * h * h
    n_scr[...] = (h / (jnp.sqrt(v) + 1e-8)).astype(BF)
    e = nn(q_scr[0], n_scr[...], None).astype(BF)
    u = nt(e, q_scr[1], None)
    out_ref[...] = u.astype(BF)
    sum_ref[...] = jnp.sum((u * u).reshape(64, 8, 4, 128), axis=(0, 2)) if False else jnp.broadcast_to(jnp.sum(u * u), (8, 128))


def block_update(g, l0, r0, ql0, qr0, v0):
    vm = pl.BlockSpec(memory_space=pltpu.VMEM)
    return pl.pallas_call(
        kernel,
        out_shape=[jax.ShapeDtypeStruct((B, B), BF), jax.ShapeDtypeStruct((8, 128), F32)],
        in_specs=[vm] * 6,
        out_specs=[vm] * 2,
        scratch_shapes=[pltpu.VMEM((2, B, B), F32), pltpu.VMEM((2, B, B), F32), pltpu.VMEM((2, B, B), BF), pltpu.VMEM((B, B), BF)],
        compiler_params=pltpu.CompilerParams(vmem_limit_bytes=60 * 2**20),
    )(g, l0, r0, ql0, qr0, v0)

FSDP = ("fsdp_0", "fsdp_1")
GROUP = ("group_0", "group_1")
FSDP_GROUP = ("fsdp_0", "fsdp_1", "group_0", "group_1")


def on_device(gradients, owners, left_factors, right_factors, left_bases, right_bases, moments):
    fsdp_count = lax.axis_size(FSDP)
    owner_row = owners[0]
    positions = jnp.arange(fsdp_count, dtype=jnp.int32)
    matches = owner_row[:, None] == positions[None, :]
    inverse = jnp.sum(jnp.where(matches, positions[:, None], 0), axis=0)
    outgoing = jnp.take(gradients, inverse, axis=0, mode="clip")
    gathered = lax.all_to_all(outgoing, FSDP, split_axis=0, concat_axis=0, tiled=True)
    gradient = gathered.reshape(B, B)
    unclipped, squares = block_update(
        gradient, left_factors[0], right_factors[0], left_bases[0], right_bases[0], moments[0]
    )
    pieces = lax.all_to_all(
        unclipped.reshape(fsdp_count, -1, B), FSDP, split_axis=0, concat_axis=0, tiled=True
    )
    total = lax.psum(squares[0, 0], FSDP_GROUP)
    count = jnp.asarray(fsdp_count * lax.axis_size(GROUP) * B * B, jnp.float32)
    scale = jnp.minimum(1.0, 0.25 * jnp.sqrt(count) / jnp.sqrt(total + 1e-06))
    return (scale * jnp.take(pieces, owner_row, axis=0, mode="clip").astype(jnp.float32)).astype(jnp.bfloat16)


def solution(mesh):
    split = Mesh(mesh.devices.reshape(4, 4, 4, 2), FSDP_GROUP)
    state = P(FSDP_GROUP, None, None)
    return jax.shard_map(
        on_device,
        mesh=split,
        in_specs=(P(GROUP, FSDP, None), P(GROUP, None), state, state, state, state, state),
        out_specs=P(GROUP, FSDP, None),
        check_vma=False,
    )
```

```python
import functools

import jax
import jax.numpy as jnp
from jax import lax
from jax.experimental import pallas as pl
from jax.experimental.pallas import tpu as pltpu
from jax.sharding import Mesh
from jax.sharding import PartitionSpec as P

SUB=8; NB=64
def sb(x, i):
    return jnp.broadcast_to(x[i:i + 1, :], x.shape)
def lanes(x, idx):
    return jnp.take_along_axis(x, idx, axis=1, mode="promise_in_bounds")
def recip(p):
    r = pl.reciprocal(p, approx=True)
    return r * (2.0 - p * r)
def invert_pair(D):
    count = NB // SUB
    sub = lax.broadcasted_iota(jnp.int32, (SUB, 128), 0)
    lane = lax.broadcasted_iota(jnp.int32, (SUB, 128), 1)
    half = lane // NB * NB
    col = lane - half
    here = [sub == i for i in range(SUB)]
    A = [D[SUB * r:SUB * (r + 1), :] for r in range(count)]
    W = [None] * count
    for s in range(count):
        base = SUB * s
        in_strip = (col >= base) & (col < base + SUB)
        unit = jnp.where(col == base + sub, 1.0, 0.0).astype(jnp.float32)
        idx = [half + (base + i) for i in range(SUB)]
        S = A[s]
        c = [lanes(S, idx[i]) for i in range(SUB)]
        S = jnp.where(in_strip, unit, S)
        for i in range(SUB):
            p = sb(c[i], i)
            rinv = recip(p)
            h = jnp.where(here[i], 1.0, -c[i])
            row = sb(S, i)
            U = row if i == 0 else jnp.where(here[i], S, U)
            rs = lax.rsqrt(p)
            scale = rs if i == 0 else jnp.where(here[i], rs, scale)
            S = jnp.where(here[i], 0.0, S) + h * (rinv * row)
            for n in range(i + 1, SUB):
                c[n] = jnp.where(here[i], 0.0, c[n]) + h * (rinv * sb(c[n], i))
        W[s] = jnp.where(col < base + SUB, U * scale, 0.0)
        z = [sb(S, i) for i in range(SUB)]
        for r in range(s + 1, count):
            X = A[r]
            acc = jnp.where(in_strip, 0.0, X)
            t0 = lanes(X, idx[0]) * z[0]
            t1 = lanes(X, idx[1]) * z[1]
            for i in range(2, SUB, 2):
                t0 = t0 + lanes(X, idx[i]) * z[i]
                t1 = t1 + lanes(X, idx[i + 1]) * z[i + 1]
            A[r] = acc - (t0 + t1)
    return jnp.concatenate(W, axis=0)


B = 512
F32 = jnp.float32
BF = jnp.bfloat16


def dot(a, b, ca, cb):
    return lax.dot_general(a, b, (((ca,), (cb,)), ((), ())), preferred_element_type=F32)


def cut(x):
    hi = x.astype(BF)
    return hi, (x - hi.astype(F32)).astype(BF)


def dot3(a, b, ca, cb):
    left = jnp.concatenate([a[0], a[0], a[1]], axis=ca)
    right = jnp.concatenate([b[0], b[1], b[0]], axis=cb)
    return dot(left, right, ca, cb)


def part(x, rows, cols):
    return x[0][rows, cols], x[1][rows, cols]


def left_half(shape):
    return lax.broadcasted_iota(jnp.int32, shape, 1) < 64


def spread(x):
    left = left_half(x.shape)
    return jnp.concatenate([jnp.where(left, x, 0.0), jnp.where(left, 0.0, x)], axis=0)


def spread2(x):
    h, l = x
    left = left_half(h.shape)
    z = jnp.zeros_like(h)
    f = lambda y: jnp.concatenate([jnp.where(left, y, z), jnp.where(left, z, y)], axis=0)
    return f(h), f(l)


def invert_128(left, right):
    half = left_half((64, 128))
    turn = lambda x: pltpu.roll(x, 64, 1)
    first = jnp.where(half, left[:64], turn(right[:64]))
    below = jnp.where(half, left[64:], turn(right[64:]))
    last = jnp.where(half, turn(left[64:]), right[64:])
    w1 = invert_pair(first)
    w1d = cut(spread(w1))
    k = dot3(cut(below), w1d, 1, 1)
    ks = cut(k)
    w2 = invert_pair(last - dot3(ks, cut(spread(k)), 1, 1))
    w21 = -dot3(cut(w2), cut(spread(dot3(ks, w1d, 1, 0))), 1, 0)
    zero = jnp.zeros((64, 128), F32)
    wl = jnp.concatenate([jnp.where(half, w1, zero), jnp.where(half, w21, turn(w2))], axis=0)
    wr = jnp.concatenate([jnp.where(half, turn(w1), zero), jnp.where(half, turn(w21), w2)], axis=0)
    return wl, wr


def kernel(g_ref, l0, r0, ql0, qr0, v0, out_ref, ph, pl_, c_scr, q_scr, n_scr):
    sides = (0, 1)
    g = g_ref[...]
    lo, hi = slice(0, 256), slice(256, 512)
    l = cut(0.95 * l0[...] + 0.05 * dot(g, g, 1, 1))
    p = dot3(l, cut(ql0[...]), 1, 0)
    ph[0], pl_[0] = cut(p)
    r = cut(0.95 * r0[...] + 0.05 * dot(g, g, 0, 0))
    p = dot3(r, cut(qr0[...]), 1, 0)
    ph[1], pl_[1] = cut(p)
    P = lambda m, c: (ph[m, :, c], pl_[m, :, c])
    for m in sides:
        c_scr[m, :, lo] = dot3(P(m, slice(0, 512)), P(m, lo), 0, 0)
        c_scr[m, hi, hi] = dot3(P(m, hi), P(m, hi), 0, 0)

    def half(o):
        a, b, e = o, o + 128, o + 256
        w1 = invert_128(c_scr[0, a:b, a:b], c_scr[1, a:b, a:b])
        w1c = [cut(w) for w in w1]
        k = [cut(dot3(cut(c_scr[m, b:e, a:b]), w1c[m], 1, 1)) for m in sides]
        w2 = invert_128(*[c_scr[m, b:e, b:e] - dot3(k[m], k[m], 1, 1) for m in sides])
        return w1, w1c, k, w2

    w1, w1c, k, w2 = half(0)
    w = []
    for m in sides:
        w21 = -dot3(cut(w2[m]), cut(dot3(k[m], w1c[m], 1, 0)), 1, 0)
        w.append(cut(jnp.concatenate([
            jnp.concatenate([w1[m], jnp.zeros((128, 128), F32)], axis=1),
            jnp.concatenate([w21, w2[m]], axis=1)], axis=0)))
    rest = []
    for m in sides:
        k = cut(dot3(cut(c_scr[m, hi, lo]), w[m], 1, 1))
        c_scr[m, hi, hi] = c_scr[m, hi, hi] - dot3(k, k, 1, 1)
        q = cut(dot3(P(m, lo), w[m], 1, 1))
        q_scr[m, :, lo] = q[0]
        ph[m, :, hi], pl_[m, :, hi] = cut(ph[m, :, hi].astype(F32) + pl_[m, :, hi].astype(F32) - dot3(q, k, 1, 1))
    w1, w1c, k, w2 = half(256)
    for m in sides:
        q = cut(dot3(P(m, slice(256, 384)), w1c[m], 1, 1))
        q_scr[m, :, 256:384] = q[0]
        s = slice(384, 512)
        y = cut(ph[m, :, s].astype(F32) + pl_[m, :, s].astype(F32) - dot3(q, k[m], 1, 1))
        q_scr[m, :, s] = dot3(y, cut(w2[m]), 1, 1).astype(BF)
    f = dot(q_scr[0], g, 0, 0).astype(BF)
    h = dot(f, q_scr[1], 1, 0)
    v = 0.95 * v0[...] + 0.05 * h * h
    n_scr[...] = (h / (jnp.sqrt(v) + 1e-8)).astype(BF)
    e = dot(q_scr[0], n_scr[...], 1, 0).astype(BF)
    u = dot(e, q_scr[1], 1, 1)
    blocks = out_ref.shape[0]
    rows = B // blocks
    for c in range(4):
        out_ref[:, rows * c:rows * (c + 1), :] = u[:, 128 * c:128 * (c + 1)].astype(BF).reshape(blocks, rows, 128)
    total = jnp.broadcast_to(jnp.sum(u * u), (8, 128))
    first = total.astype(BF)
    second = (total - first.astype(F32)).astype(BF)
    third = (total - first.astype(F32) - second.astype(F32)).astype(BF)
    row = lax.broadcasted_iota(jnp.int32, (8, 128), 0)
    tail = jnp.where(row == 0, first.astype(F32), jnp.where(row == 1, second.astype(F32), jnp.where(row == 2, third.astype(F32), 0.0)))
    out_ref[:, 4 * rows:, :] = jnp.broadcast_to(tail.astype(BF)[None], (blocks, 8, 128))


def block_update(g, l0, r0, ql0, qr0, v0):
    vm = pl.BlockSpec(memory_space=pltpu.VMEM)
    return pl.pallas_call(
        kernel,
        out_shape=jax.ShapeDtypeStruct((16, B // 4 + 8, 128), BF),
        in_specs=[vm] * 6,
        out_specs=vm,
        name="update",
        scratch_shapes=[pltpu.VMEM((2, B, B), BF), pltpu.VMEM((2, B, B), BF), pltpu.VMEM((2, B, B), F32), pltpu.VMEM((2, B, B), BF), pltpu.VMEM((B, B), BF)],
        compiler_params=pltpu.CompilerParams(vmem_limit_bytes=24 * 2**20),
    )(g, l0, r0, ql0, qr0, v0)

FSDP = ("fsdp_0", "fsdp_1")
GROUP = ("group_0", "group_1")
FSDP_GROUP = ("fsdp_0", "fsdp_1", "group_0", "group_1")


def finish_kernel(owner_ref, total_ref, pieces_ref, out_ref, *, count):
    total = jnp.sum(total_ref[...], axis=0, keepdims=True)
    scale = jnp.minimum(1.0, 0.25 * jnp.sqrt(jnp.float32(count)) / jnp.sqrt(total + 1e-06))
    rows = out_ref.shape[1]
    scale = jnp.broadcast_to(scale, (rows, 128))
    for j in range(out_ref.shape[0]):
        owner = owner_ref[j]
        for c in range(B // 128):
            x = pieces_ref[owner, rows * c:rows * (c + 1), :].astype(jnp.float32)
            out_ref[j, :, 128 * c:128 * (c + 1)] = (scale * x).astype(jnp.bfloat16)


def finish(owner_row, totals, pieces, count):
    vm = pl.BlockSpec(memory_space=pltpu.VMEM)
    blocks = pieces.shape[0]
    return pl.pallas_call(
        functools.partial(finish_kernel, count=count),
        out_shape=jax.ShapeDtypeStruct((blocks, B // blocks, B), jnp.bfloat16),
        in_specs=[pl.BlockSpec(memory_space=pltpu.SMEM), vm, vm],
        out_specs=vm,
        name="finish",
        compiler_params=pltpu.CompilerParams(vmem_limit_bytes=4 * 2**20),
    )(owner_row, totals, pieces)


def on_device(gradients, owners, left_factors, right_factors, left_bases, right_bases, moments):
    fsdp_count, group_count = lax.axis_size(FSDP), lax.axis_size(GROUP)
    owner_row = owners[0]
    positions = jnp.arange(fsdp_count, dtype=jnp.int32)
    matches = owner_row[:, None] == positions[None, :]
    inverse = jnp.sum(jnp.where(matches, positions[:, None], 0), axis=0)
    outgoing = jnp.take(gradients, inverse, axis=0, mode="clip")
    gathered = lax.all_to_all(outgoing, FSDP, split_axis=0, concat_axis=0, tiled=True)
    packed = block_update(
        gathered.reshape(B, B), left_factors[0], right_factors[0], left_bases[0], right_bases[0], moments[0]
    )
    pieces = lax.all_to_all(packed, FSDP, split_axis=0, concat_axis=0, tiled=True)
    squares = jnp.sum(pieces[:, B // 4:B // 4 + 3, :].astype(jnp.float32), axis=(0, 1))
    totals = lax.all_to_all(
        jnp.broadcast_to(squares[None], (group_count, 128)), GROUP, split_axis=0, concat_axis=0, tiled=True
    )
    return finish(owner_row, totals, pieces, fsdp_count * group_count * B * B)


def solution(mesh):
    split = Mesh(mesh.devices.reshape(4, 4, 4, 2), FSDP_GROUP)
    state = P(FSDP_GROUP, None, None)
    return jax.shard_map(
        on_device,
        mesh=split,
        in_specs=(P(GROUP, FSDP, None), P(GROUP, None), state, state, state, state, state),
        out_specs=P(GROUP, FSDP, None),
        check_vma=False,
    )
```

```python
import functools

import jax
import jax.numpy as jnp
from jax import lax
from jax.experimental import pallas as pl
from jax.experimental.pallas import tpu as pltpu
from jax.sharding import Mesh
from jax.sharding import PartitionSpec as P


B = 512
SUB = 8
NB = 64
F32 = jnp.float32
BF = jnp.bfloat16
SIDES = (0, 1)
BASES = B // NB


def dot(a, b, ca, cb):
    return lax.dot_general(a, b, (((ca,), (cb,)), ((), ())), preferred_element_type=F32)


def cut(x):
    hi = x.astype(BF)
    return hi, (x - hi.astype(F32)).astype(BF)


def join(x):
    return x[0].astype(F32) + x[1].astype(F32)


def dot3(a, b, ca, cb):
    left = jnp.concatenate([a[0], a[0], a[1]], axis=ca)
    right = jnp.concatenate([b[0], b[1], b[0]], axis=cb)
    return dot(left, right, ca, cb)


def turn(x):
    return pltpu.roll(x, NB, 1)


def left_half(rows):
    return lax.broadcasted_iota(jnp.int32, (rows, 128), 1) < NB


def spread(x):
    left = left_half(x.shape[0])
    return jnp.concatenate([jnp.where(left, x, 0.0), jnp.where(left, 0.0, x)], axis=0)


def sb(x, i):
    return jnp.broadcast_to(x[i:i + 1, :], x.shape)


def lanes(x, idx):
    return jnp.take_along_axis(x, idx, axis=1, mode="promise_in_bounds")


def recip(p):
    r = pl.reciprocal(p, approx=True)
    return r * (2.0 - p * r)


def invert_pair(D, fill):
    count = NB // SUB
    sub = lax.broadcasted_iota(jnp.int32, (SUB, 128), 0)
    lane = lax.broadcasted_iota(jnp.int32, (SUB, 128), 1)
    half = lane // NB * NB
    col = lane - half
    here = [sub == i for i in range(SUB)]
    A = [D[SUB * r:SUB * (r + 1), :] for r in range(count)]
    W = [None] * count
    for s in range(count):
        base = SUB * s
        in_strip = (col >= base) & (col < base + SUB)
        unit = jnp.where(col == base + sub, 1.0, 0.0).astype(F32)
        idx = [half + (base + i) for i in range(SUB)]
        S = A[s]
        c = [lanes(S, idx[i]) for i in range(SUB)]
        S = jnp.where(in_strip, unit, S)
        for i in range(SUB):
            p = sb(c[i], i)
            rinv = recip(p)
            h = jnp.where(here[i], 1.0, -c[i])
            row = sb(S, i)
            U = row if i == 0 else jnp.where(here[i], S, U)
            rs = lax.rsqrt(p)
            scale = rs if i == 0 else jnp.where(here[i], rs, scale)
            S = jnp.where(here[i], 0.0, S) + h * (rinv * row)
            for n in range(i + 1, SUB):
                c[n] = jnp.where(here[i], 0.0, c[n]) + h * (rinv * sb(c[n], i))
        W[s] = jnp.where(col < base + SUB, U * scale, 0.0)
        z = [sb(S, i) for i in range(SUB)]
        for r in range(s + 1, count):
            X = A[r]
            acc = jnp.where(in_strip, 0.0, X)
            t0 = lanes(X, idx[0]) * z[0]
            t1 = lanes(X, idx[1]) * z[1]
            for i in range(2, SUB, 2):
                t0 = t0 + lanes(X, idx[i]) * z[i]
                t1 = t1 + lanes(X, idx[i + 1]) * z[i + 1]
            A[r] = acc - (t0 + t1)
        fill()
    return jnp.concatenate(W, axis=0)


class Tasks:
    def __init__(self):
        self.open = []
        self.slots = BASES * (NB // SUB)
        self.base = 0

    def add(self, run, cost, last, needs=()):
        task = [run, cost, last, needs]
        self.open.append(task)
        return task

    def do(self, task):
        if task in self.open:
            self.open.remove(task)
            for other in task[3]:
                self.do(other)
            task[0]()

    def fill(self):
        self.slots -= 1
        left = self.slots % (NB // SUB) + 1
        urgent = sum(t[1] for t in self.open if t[2] <= self.base) / left
        even = sum(t[1] for t in self.open) / (self.slots + 1)
        share, done = max(urgent, even), 0.0
        while self.open and done < share:
            task = min(self.open, key=lambda t: t[2])
            done += task[1]
            self.do(task)

    def end_base(self):
        for task in [t for t in self.open if t[2] <= self.base]:
            self.do(task)
        self.base += 1

    def flush(self):
        while self.open:
            self.do(self.open[0])


def rows_of(i, n=128):
    return slice(n * i, n * (i + 1))


def kernel(g_ref, l0, r0, ql_hbm, qr_hbm, v_hbm, out_ref,
           basis, v0, lh, ll, ph, pl_, cp, kh, kl, uh, ul, q_scr, f_scr, n_scr, sem):
    copies = [pltpu.make_async_copy(ql_hbm.at[0], basis.at[0], sem.at[0]),
              pltpu.make_async_copy(qr_hbm.at[0], basis.at[1], sem.at[1]),
              pltpu.make_async_copy(v_hbm.at[0], v0, sem.at[2])]
    for copy in copies:
        copy.start()
    tasks = Tasks()
    P = lambda m, r, c: (ph[m, r, c], pl_[m, r, c])
    every = slice(0, B)

    def project(m, r, c):
        ph[m, r, c], pl_[m, r, c] = cut(dot3((lh[m, r, :], ll[m, r, :]), cut(basis[m, :, c]), 1, 0))

    def correlate(i, c):
        both = [dot3(P(m, every, rows_of(i)), P(m, every, c), 0, 0) for m in SIDES]
        half = left_half(128)
        for j in range((c.stop - c.start) // 128):
            l, r = (x[:, rows_of(j)] for x in both)
            at = 2 * c.start + 256 * j
            cp[rows_of(i), at:at + 128] = jnp.where(half, l, turn(r))
            cp[rows_of(i), at + 128:at + 256] = jnp.where(half, turn(l), r)

    lo, hi = slice(0, 256), slice(256, 512)
    for m, old in ((0, l0), (1, r0)):
        g = g_ref[...]
        lh[m], ll[m] = cut(0.95 * old[...] + 0.05 * dot(g, g, 1 - m, 1 - m))
    for m in SIDES:
        copies[m].wait()
        project(m, every, lo)
    correlate(0, slice(0, 128))
    c_low = [tasks.add(lambda: correlate(1, lo), 900, 0)]
    p_high = [tasks.add(lambda m=m, i=i: project(m, rows_of(i), hi), 220, 1) for m in SIDES for i in range(4)]
    c_low += [tasks.add(lambda i=i: correlate(i, lo), 900, 1, p_high) for i in (2, 3)]
    c_high = [tasks.add(lambda: correlate(2, slice(256, 384)), 500, 1, p_high),
              tasks.add(lambda: correlate(3, hi), 900, 1, p_high)]

    def column(b):
        return slice(128 * b, 128 * (b + 1))

    K = lambda b, r: (kh[r, column(b)], kl[r, column(b)])
    w = [None] * BASES
    wd = [None] * BASES
    product = [None] * BASES
    w128 = [None] * 4
    k_rest = [None] * BASES
    move = [None] * 4

    def below(b, r):
        kh[r, column(b)], kl[r, column(b)] = cut(dot3(cut(cp[r, column(b)]), wd[b], 1, 1))

    def update(b, j, r):
        cp[r, column(j)] = cp[r, column(j)] - dot3(K(b, r), cut(spread(join(K(b, rows_of(j, NB))))), 1, 1)

    def assemble(k):
        b = 2 * k
        half = left_half(NB)
        w1, w2 = w[b], w[b + 1]
        w21 = -dot3(cut(w2), cut(spread(product[b])), 1, 0)
        w128[k] = [cut(jnp.concatenate([jnp.where(half, w1, 0.0), jnp.where(half, w21, turn(w2))], axis=0)),
                   cut(jnp.concatenate([jnp.where(half, turn(w1), 0.0), jnp.where(half, turn(w21), w2)], axis=0))]

    def separate(k):
        r = slice(128 * (k + 1), B)
        half = left_half(B - r.start)
        a, c = join(K(2 * k, r)), join(K(2 * k + 1, r))
        uh[0, r, rows_of(k)], ul[0, r, rows_of(k)] = cut(jnp.where(half, a, turn(c)))
        uh[1, r, rows_of(k)], ul[1, r, rows_of(k)] = cut(jnp.where(half, turn(a), c))

    def solve(k, m, r):
        q = cut(dot3(P(m, r, rows_of(k)), w128[k][m], 1, 1))
        q_scr[m, r, rows_of(k)] = q[0]
        if k < 3:
            c = slice(128 * (k + 1), B)
            ph[m, r, c], pl_[m, r, c] = cut(
                join(P(m, r, c)) - dot3(q, (uh[m, c, rows_of(k)], ul[m, c, rows_of(k)]), 1, 1))

    def rotate(k):
        f_scr[rows_of(k), :] = dot(q_scr[0, :, rows_of(k)], g_ref[...], 0, 0).astype(BF)

    solved = []
    d = cp[0:NB, 0:128]
    for b in range(BASES):
        w[b] = invert_pair(d, tasks.fill)
        tasks.end_base()
        wd[b] = cut(spread(w[b]))
        if b + 1 < BASES:
            r = rows_of(b + 1, NB)
            below(b, r)
            x = join(K(b, r))
            d = cp[r, column(b + 1)] - dot3(cut(x), cut(spread(x)), 1, 1)
        if b % 2 == 0:
            def multiply(b=b):
                product[b] = dot3(K(b, rows_of(b + 1, NB)), wd[b], 1, 0)
            tasks.add(multiply, 100, b + 1)
        if b + 2 < BASES:
            rest = slice(NB * (b + 2), B)
            k_rest[b] = tasks.add(lambda b=b, rest=rest: below(b, rest), (B - rest.start) * 0.6, b + 1, c_low)
            for j in range(b + 1, BASES):
                r = slice(NB * max(j, b + 2), B)
                tasks.add(lambda b=b, j=j, r=r: update(b, j, r), (B - r.start) * 0.6, max(j - 1, b + 1) if j > b + 2 else b + 1,
                          [k_rest[b]] + (c_high if j >= 4 and b < 2 else []))
        if b % 2:
            k = b // 2
            assembled = tasks.add(lambda k=k: assemble(k), 150, b + 2)
            needs = [assembled]
            if k < 3:
                needs.append(tasks.add(lambda k=k: separate(k), 200, b + 2, [k_rest[b - 1], k_rest[b]] if k_rest[b] else [k_rest[b - 1]]))
            solved = [tasks.add(lambda k=k, m=m, i=i: solve(k, m, rows_of(i)), 220 if k < 3 else 100, b + 2, needs + solved + p_high)
                      for m in SIDES for i in range(4)]
            tasks.add(lambda k=k: rotate(k), 300, b + 2, solved)
    tasks.flush()
    copies[2].wait()
    h = dot(f_scr[...], q_scr[1], 1, 0)
    v = 0.95 * v0[...] + 0.05 * h * h
    n_scr[...] = (h / (jnp.sqrt(v) + 1e-8)).astype(BF)
    e = dot(q_scr[0], n_scr[...], 1, 0).astype(BF)
    u = dot(e, q_scr[1], 1, 1)
    blocks = out_ref.shape[0]
    rows = B // blocks
    for c in range(4):
        out_ref[:, rows * c:rows * (c + 1), :] = u[:, 128 * c:128 * (c + 1)].astype(BF).reshape(blocks, rows, 128)
    total = jnp.broadcast_to(jnp.sum(u * u), (8, 128))
    first = total.astype(BF).astype(F32)
    second = (total - first).astype(BF).astype(F32)
    third = total - first - second
    row = lax.broadcasted_iota(jnp.int32, (8, 128), 0)
    tail = jnp.where(row == 0, first, jnp.where(row == 1, second, jnp.where(row == 2, third, 0.0)))
    out_ref[:, 4 * rows:, :] = jnp.broadcast_to(tail.astype(BF)[None], (blocks, 8, 128))


def block_update(g, l0, r0, ql0, qr0, v0):
    vm = pl.BlockSpec(memory_space=pltpu.VMEM)
    hbm = pl.BlockSpec(memory_space=pl.ANY)
    return pl.pallas_call(
        kernel,
        out_shape=jax.ShapeDtypeStruct((16, B // 4 + 8, 128), BF),
        in_specs=[vm] * 3 + [hbm] * 3,
        out_specs=vm,
        name="update",
        scratch_shapes=[pltpu.VMEM((2, B, B), F32), pltpu.VMEM((B, B), F32)]
        + [pltpu.VMEM((2, B, B), BF)] * 4
        + [pltpu.VMEM((B, 2 * B), F32), pltpu.VMEM((B, 2 * B), BF), pltpu.VMEM((B, 2 * B), BF)]
        + [pltpu.VMEM((2, B, B), BF)] * 3
        + [pltpu.VMEM((B, B), BF)] * 2
        + [pltpu.SemaphoreType.DMA((3,))],
        compiler_params=pltpu.CompilerParams(vmem_limit_bytes=24 * 2**20),
    )(g, l0, r0, ql0, qr0, v0)

FSDP = ("fsdp_0", "fsdp_1")
GROUP = ("group_0", "group_1")
FSDP_GROUP = ("fsdp_0", "fsdp_1", "group_0", "group_1")


def finish_kernel(owner_ref, total_ref, pieces_ref, out_ref, *, count):
    total = jnp.sum(total_ref[...], axis=0, keepdims=True)
    scale = jnp.minimum(1.0, 0.25 * jnp.sqrt(jnp.float32(count)) / jnp.sqrt(total + 1e-06))
    rows = out_ref.shape[1]
    scale = jnp.broadcast_to(scale, (rows, 128))
    for j in range(out_ref.shape[0]):
        owner = owner_ref[j]
        for c in range(B // 128):
            x = pieces_ref[owner, rows * c:rows * (c + 1), :].astype(jnp.float32)
            out_ref[j, :, 128 * c:128 * (c + 1)] = (scale * x).astype(jnp.bfloat16)


def finish(owner_row, totals, pieces, count):
    vm = pl.BlockSpec(memory_space=pltpu.VMEM)
    blocks = pieces.shape[0]
    return pl.pallas_call(
        functools.partial(finish_kernel, count=count),
        out_shape=jax.ShapeDtypeStruct((blocks, B // blocks, B), jnp.bfloat16),
        in_specs=[pl.BlockSpec(memory_space=pltpu.SMEM), vm, vm],
        out_specs=vm,
        name="finish",
        compiler_params=pltpu.CompilerParams(vmem_limit_bytes=4 * 2**20),
    )(owner_row, totals, pieces)


def on_device(gradients, owners, left_factors, right_factors, left_bases, right_bases, moments):
    fsdp_count, group_count = lax.axis_size(FSDP), lax.axis_size(GROUP)
    owner_row = owners[0]
    positions = jnp.arange(fsdp_count, dtype=jnp.int32)
    matches = owner_row[:, None] == positions[None, :]
    inverse = jnp.sum(jnp.where(matches, positions[:, None], 0), axis=0)
    outgoing = jnp.take(gradients, inverse, axis=0, mode="clip")
    gathered = lax.all_to_all(outgoing, FSDP, split_axis=0, concat_axis=0, tiled=True)
    packed = block_update(
        gathered.reshape(B, B), left_factors[0], right_factors[0], left_bases, right_bases, moments
    )
    pieces = lax.all_to_all(packed, FSDP, split_axis=0, concat_axis=0, tiled=True)
    squares = jnp.sum(pieces[:, B // 4:B // 4 + 3, :].astype(jnp.float32), axis=(0, 1))
    totals = lax.all_to_all(
        jnp.broadcast_to(squares[None], (group_count, 128)), GROUP, split_axis=0, concat_axis=0, tiled=True
    )
    return finish(owner_row, totals, pieces, fsdp_count * group_count * B * B)


def solution(mesh):
    split = Mesh(mesh.devices.reshape(4, 4, 4, 2), FSDP_GROUP)
    state = P(FSDP_GROUP, None, None)
    return jax.shard_map(
        on_device,
        mesh=split,
        in_specs=(P(GROUP, FSDP, None), P(GROUP, None), state, state, state, state, state),
        out_specs=P(GROUP, FSDP, None),
        check_vma=False,
    )
```

```python
import functools

import jax
import jax.numpy as jnp
from jax import lax
from jax.experimental import pallas as pl
from jax.experimental.pallas import tpu as pltpu
from jax.sharding import Mesh
from jax.sharding import PartitionSpec as P


B = 512
SUB = 8
NB = 64
F32 = jnp.float32
BF = jnp.bfloat16
SIDES = (0, 1)
BASES = B // NB


def dot(a, b, ca, cb):
    return lax.dot_general(a, b, (((ca,), (cb,)), ((), ())), preferred_element_type=F32)


def cut(x):
    hi = x.astype(BF)
    return hi, (x - hi.astype(F32)).astype(BF)


def join(x):
    return x[0].astype(F32) + x[1].astype(F32)


def dot3(a, b, ca, cb):
    left = jnp.concatenate([a[0], a[0], a[1]], axis=ca)
    right = jnp.concatenate([b[0], b[1], b[0]], axis=cb)
    return dot(left, right, ca, cb)


def turn(x):
    return pltpu.roll(x, NB, 1)


def left_half(rows):
    return lax.broadcasted_iota(jnp.int32, (rows, 128), 1) < NB


def spread(x):
    left = left_half(x.shape[0])
    return jnp.concatenate([jnp.where(left, x, 0.0), jnp.where(left, 0.0, x)], axis=0)


def sb(x, i):
    return jnp.broadcast_to(x[i:i + 1, :], x.shape)


def lanes(x, idx):
    return jnp.take_along_axis(x, idx, axis=1, mode="promise_in_bounds")


def recip(p):
    r = pl.reciprocal(p, approx=True)
    return r, 2.0 - p * r


def invert_pair(D, fill):
    count = NB // SUB
    sub = lax.broadcasted_iota(jnp.int32, (SUB, 128), 0)
    lane = lax.broadcasted_iota(jnp.int32, (SUB, 128), 1)
    half = lane // NB * NB
    col = lane - half
    idx = [half + i for i in range(NB)]
    A = [D[SUB * r:SUB * (r + 1), :] for r in range(count)]
    W = [None] * count
    c = [lanes(A[0], idx[i]) for i in range(SUB)]
    for s in range(count):
        base = SUB * s
        more = s + 1 < count
        in_strip = (col >= base) & (col < base + SUB)
        unit = jnp.where(col == base + sub, 1.0, 0.0).astype(F32)
        ahead = [lanes(A[s], idx[base + SUB + j]) for j in range(SUB)] if more else []
        S = jnp.where(in_strip, unit, A[s])
        U = S
        scale = S
        for i in range(0, SUB, 2):
            at0, at1 = sub == i, sub == i + 1
            other = (sub < i) | (sub > i + 1)
            a, b, d = sb(c[i], i), sb(c[i], i + 1), sb(c[i + 1], i + 1)
            det = a * d - b * b
            rdet, fix = recip(det)
            m0 = jnp.where(other, -c[i], jnp.where(at0, 1.0, 0.0))
            m1 = jnp.where(other, -c[i + 1], jnp.where(at1, 1.0, 0.0))
            e0 = m0 * d - m1 * b
            e1 = m1 * a - m0 * b

            def eliminate(x):
                keep = jnp.where(other, x, 0.0)
                return keep + fix * (rdet * (e0 * sb(x, i) + e1 * sb(x, i + 1)))

            ra, fix_a = recip(a)
            ra = ra * fix_a
            row0, row1 = sb(S, i), sb(S, i + 1)
            U = jnp.where(at0, row0, jnp.where(at1, row1 - (b * ra) * row0, U))
            scale = jnp.where(at0, lax.rsqrt(a), jnp.where(at1, lax.rsqrt(det * ra), scale))
            S = eliminate(S)
            for n in range(i + 2, SUB):
                c[n] = eliminate(c[n])
            ahead = [eliminate(x) for x in ahead]
        W[s] = jnp.where(col < base + SUB, U * scale, 0.0)
        z = [sb(S, i) for i in range(SUB)]
        for r in range(s + 1, count):
            X = A[r]
            x = [lanes(X, idx[base + i]) for i in range(SUB)]
            if r == s + 1:
                c = []
                for j in range(SUB):
                    t = [x[i] * sb(ahead[j], i) for i in range(SUB)]
                    c.append(lanes(X, idx[base + SUB + j]) - (((t[0] + t[1]) + (t[2] + t[3])) + ((t[4] + t[5]) + (t[6] + t[7]))))
            t = [x[i] * z[i] for i in range(SUB)]
            A[r] = jnp.where(in_strip, 0.0, X) - (((t[0] + t[1]) + (t[2] + t[3])) + ((t[4] + t[5]) + (t[6] + t[7])))
        fill()
    return jnp.concatenate(W, axis=0)


class Tasks:
    def __init__(self):
        self.open = []
        self.slots = BASES * (NB // SUB)
        self.base = 0

    def add(self, run, cost, last, needs=()):
        task = [run, cost, last, needs]
        self.open.append(task)
        return task

    def do(self, task):
        if task in self.open:
            self.open.remove(task)
            for other in task[3]:
                self.do(other)
            task[0]()

    def fill(self):
        self.slots -= 1
        left = self.slots % (NB // SUB) + 1
        urgent = sum(t[1] for t in self.open if t[2] <= self.base) / left
        even = sum(t[1] for t in self.open) / (self.slots + 1)
        share, done = max(urgent, even), 0.0
        while self.open and done < share:
            task = min(self.open, key=lambda t: t[2])
            done += task[1]
            self.do(task)

    def end_base(self):
        for task in [t for t in self.open if t[2] <= self.base]:
            self.do(task)
        self.base += 1

    def flush(self):
        while self.open:
            self.do(self.open[0])


def rows_of(i, n=128):
    return slice(n * i, n * (i + 1))


def kernel(g_ref, l_hbm, r_hbm, ql_hbm, qr_hbm, v_hbm, out_ref,
           old, basis, v0, lh, ll, ph, pl_, cp, kh, kl, uh, ul, q_scr, f_scr, n_scr, sem):
    copies = [pltpu.make_async_copy(source.at[0], target, sem.at[i]) for i, (source, target) in enumerate((
        (l_hbm, old.at[0]), (ql_hbm, basis.at[0]), (r_hbm, old.at[1]), (qr_hbm, basis.at[1]), (v_hbm, v0)))]
    for copy in copies:
        copy.start()
    tasks = Tasks()
    P = lambda m, r, c: (ph[m, r, c], pl_[m, r, c])
    every = slice(0, B)

    def project(m, r, c):
        ph[m, r, c], pl_[m, r, c] = cut(dot3((lh[m, r, :], ll[m, r, :]), cut(basis[m, :, c]), 1, 0))

    def correlate(i, c):
        both = [dot3(P(m, every, rows_of(i)), P(m, every, c), 0, 0) for m in SIDES]
        half = left_half(128)
        for j in range((c.stop - c.start) // 128):
            l, r = (x[:, rows_of(j)] for x in both)
            at = 2 * c.start + 256 * j
            cp[rows_of(i), at:at + 128] = jnp.where(half, l, turn(r))
            cp[rows_of(i), at + 128:at + 256] = jnp.where(half, turn(l), r)

    lo, hi = slice(0, 256), slice(256, 512)
    for m in SIDES:
        g = g_ref[...]
        gram = 0.05 * dot(g, g, 1 - m, 1 - m)
        copies[2 * m].wait()
        lh[m], ll[m] = cut(0.95 * old[m] + gram)
        copies[2 * m + 1].wait()
        project(m, every, lo)
    correlate(0, slice(0, 128))
    c_low = [tasks.add(lambda: correlate(1, lo), 900, 0)]
    p_high = [tasks.add(lambda m=m: project(m, every, hi), 880, 1) for m in SIDES]
    c_low += [tasks.add(lambda i=i: correlate(i, lo), 900, 1, p_high) for i in (2, 3)]
    c_high = [tasks.add(lambda: correlate(2, slice(256, 384)), 500, 1, p_high),
              tasks.add(lambda: correlate(3, hi), 900, 1, p_high)]

    def column(b):
        return slice(128 * b, 128 * (b + 1))

    K = lambda b, r: (kh[r, column(b)], kl[r, column(b)])
    w = [None] * BASES
    wd = [None] * BASES
    product = [None] * BASES
    w128 = [None] * 4
    k_rest = [None] * BASES
    move = [None] * 4

    def below(b, r):
        kh[r, column(b)], kl[r, column(b)] = cut(dot3(cut(cp[r, column(b)]), wd[b], 1, 1))

    def update(b, first, end, r):
        pairs = [cut(spread(join(K(b, rows_of(j, NB))))) for j in range(first, end)]
        right = [jnp.concatenate([x[i] for x in pairs], axis=0) for i in (0, 1)]
        c = slice(128 * first, 128 * end)
        cp[r, c] = cp[r, c] - dot3(K(b, r), right, 1, 1)

    def assemble(k):
        b = 2 * k
        half = left_half(NB)
        w1, w2 = w[b], w[b + 1]
        w21 = -dot3(cut(w2), cut(spread(product[b])), 1, 0)
        w128[k] = [cut(jnp.concatenate([jnp.where(half, w1, 0.0), jnp.where(half, w21, turn(w2))], axis=0)),
                   cut(jnp.concatenate([jnp.where(half, turn(w1), 0.0), jnp.where(half, turn(w21), w2)], axis=0))]

    def separate(k):
        r = slice(128 * (k + 1), B)
        half = left_half(B - r.start)
        a, c = join(K(2 * k, r)), join(K(2 * k + 1, r))
        uh[0, r, rows_of(k)], ul[0, r, rows_of(k)] = cut(jnp.where(half, a, turn(c)))
        uh[1, r, rows_of(k)], ul[1, r, rows_of(k)] = cut(jnp.where(half, turn(a), c))

    def solve(k, m, r):
        q = cut(dot3(P(m, r, rows_of(k)), w128[k][m], 1, 1))
        q_scr[m, r, rows_of(k)] = q[0]
        if k < 3:
            c = slice(128 * (k + 1), B)
            ph[m, r, c], pl_[m, r, c] = cut(
                join(P(m, r, c)) - dot3(q, (uh[m, c, rows_of(k)], ul[m, c, rows_of(k)]), 1, 1))

    def rotate(k):
        f_scr[rows_of(k), :] = dot(q_scr[0, :, rows_of(k)], g_ref[...], 0, 0).astype(BF)

    solved = []
    d = cp[0:NB, 0:128]
    for b in range(BASES):
        w[b] = invert_pair(d, tasks.fill)
        tasks.end_base()
        wd[b] = cut(spread(w[b]))
        if b + 1 < BASES:
            r = rows_of(b + 1, NB)
            below(b, r)
            x = join(K(b, r))
            d = cp[r, column(b + 1)] - dot3(cut(x), cut(spread(x)), 1, 1)
        if b % 2 == 0:
            def multiply(b=b):
                product[b] = dot3(K(b, rows_of(b + 1, NB)), wd[b], 1, 0)
            tasks.add(multiply, 100, b + 1)
        if b + 2 < BASES:
            rest = slice(NB * (b + 2), B)
            k_rest[b] = tasks.add(lambda b=b, rest=rest: below(b, rest), (B - rest.start) * 0.6, b + 1, c_low)
            tasks.add(lambda b=b, rest=rest: update(b, b + 1, b + 3, rest), 300 + B - rest.start, b + 1, [k_rest[b]])
            if b + 3 < BASES:
                far = slice(NB * (b + 3), B)
                tasks.add(lambda b=b, far=far: update(b, b + 3, BASES, far), 300 + (B - far.start) * (BASES - b - 3) * 0.5, b + 2,
                          [k_rest[b]] + (c_high if b < 2 else []))
        if b % 2:
            k = b // 2
            assembled = tasks.add(lambda k=k: assemble(k), 150, b + 2)
            needs = [assembled]
            if k < 3:
                needs.append(tasks.add(lambda k=k: separate(k), 200, b + 2, [k_rest[b - 1], k_rest[b]] if k_rest[b] else [k_rest[b - 1]]))
            solved = [tasks.add(lambda k=k, m=m: solve(k, m, every), 900 if k < 3 else 400, b + 2, needs + solved + p_high)
                      for m in SIDES]
            tasks.add(lambda k=k: rotate(k), 300, b + 2, solved)
    tasks.flush()
    copies[4].wait()
    h = dot(f_scr[...], q_scr[1], 1, 0)
    v = 0.95 * v0[...] + 0.05 * h * h
    n_scr[...] = (h / (jnp.sqrt(v) + 1e-8)).astype(BF)
    e = dot(q_scr[0], n_scr[...], 1, 0).astype(BF)
    u = dot(e, q_scr[1], 1, 1)
    blocks = out_ref.shape[0]
    rows = B // blocks
    for c in range(4):
        out_ref[:, rows * c:rows * (c + 1), :] = u[:, 128 * c:128 * (c + 1)].astype(BF).reshape(blocks, rows, 128)
    total = jnp.broadcast_to(jnp.sum(u * u), (8, 128))
    first = total.astype(BF).astype(F32)
    second = (total - first).astype(BF).astype(F32)
    third = total - first - second
    row = lax.broadcasted_iota(jnp.int32, (8, 128), 0)
    tail = jnp.where(row == 0, first, jnp.where(row == 1, second, jnp.where(row == 2, third, 0.0)))
    out_ref[:, 4 * rows:, :] = jnp.broadcast_to(tail.astype(BF)[None], (blocks, 8, 128))


def block_update(g, l0, r0, ql0, qr0, v0):
    vm = pl.BlockSpec(memory_space=pltpu.VMEM)
    hbm = pl.BlockSpec(memory_space=pl.ANY)
    return pl.pallas_call(
        kernel,
        out_shape=jax.ShapeDtypeStruct((16, B // 4 + 8, 128), BF),
        in_specs=[vm] + [hbm] * 5,
        out_specs=vm,
        name="update",
        scratch_shapes=[pltpu.VMEM((2, B, B), F32)] * 2 + [pltpu.VMEM((B, B), F32)]
        + [pltpu.VMEM((2, B, B), BF)] * 4
        + [pltpu.VMEM((B, 2 * B), F32), pltpu.VMEM((B, 2 * B), BF), pltpu.VMEM((B, 2 * B), BF)]
        + [pltpu.VMEM((2, B, B), BF)] * 3
        + [pltpu.VMEM((B, B), BF)] * 2
        + [pltpu.SemaphoreType.DMA((5,))],
        compiler_params=pltpu.CompilerParams(vmem_limit_bytes=52 * 2**20),
    )(g, l0, r0, ql0, qr0, v0)

FSDP = ("fsdp_0", "fsdp_1")
GROUP = ("group_0", "group_1")
FSDP_GROUP = ("fsdp_0", "fsdp_1", "group_0", "group_1")


def finish_kernel(owner_ref, total_ref, pieces_ref, out_ref, *, count):
    total = jnp.sum(total_ref[...], axis=0, keepdims=True)
    scale = jnp.minimum(1.0, 0.25 * jnp.sqrt(jnp.float32(count)) / jnp.sqrt(total + 1e-06))
    rows = out_ref.shape[1]
    scale = jnp.broadcast_to(scale, (rows, 128))
    for j in range(out_ref.shape[0]):
        owner = owner_ref[j]
        for c in range(B // 128):
            x = pieces_ref[owner, rows * c:rows * (c + 1), :].astype(jnp.float32)
            out_ref[j, :, 128 * c:128 * (c + 1)] = (scale * x).astype(jnp.bfloat16)


def finish(owner_row, totals, pieces, count):
    vm = pl.BlockSpec(memory_space=pltpu.VMEM)
    blocks = pieces.shape[0]
    return pl.pallas_call(
        functools.partial(finish_kernel, count=count),
        out_shape=jax.ShapeDtypeStruct((blocks, B // blocks, B), jnp.bfloat16),
        in_specs=[pl.BlockSpec(memory_space=pltpu.SMEM), vm, vm],
        out_specs=vm,
        name="finish",
        compiler_params=pltpu.CompilerParams(vmem_limit_bytes=4 * 2**20),
    )(owner_row, totals, pieces)


def on_device(gradients, owners, left_factors, right_factors, left_bases, right_bases, moments):
    fsdp_count, group_count = lax.axis_size(FSDP), lax.axis_size(GROUP)
    owner_row = owners[0]
    positions = jnp.arange(fsdp_count, dtype=jnp.int32)
    matches = owner_row[:, None] == positions[None, :]
    inverse = jnp.sum(jnp.where(matches, positions[:, None], 0), axis=0)
    outgoing = jnp.take(gradients, inverse, axis=0, mode="clip")
    gathered = lax.all_to_all(outgoing, FSDP, split_axis=0, concat_axis=0, tiled=True)
    packed = block_update(
        gathered.reshape(B, B), left_factors, right_factors, left_bases, right_bases, moments
    )
    pieces = lax.all_to_all(packed, FSDP, split_axis=0, concat_axis=0, tiled=True)
    squares = jnp.sum(pieces[:, B // 4:B // 4 + 3, :].astype(jnp.float32), axis=(0, 1))
    totals = lax.all_to_all(
        jnp.broadcast_to(squares[None], (group_count, 128)), GROUP, split_axis=0, concat_axis=0, tiled=True
    )
    return finish(owner_row, totals, pieces, fsdp_count * group_count * B * B)


def solution(mesh):
    split = Mesh(mesh.devices.reshape(4, 4, 4, 2), FSDP_GROUP)
    state = P(FSDP_GROUP, None, None)
    return jax.shard_map(
        on_device,
        mesh=split,
        in_specs=(P(GROUP, FSDP, None), P(GROUP, None), state, state, state, state, state),
        out_specs=P(GROUP, FSDP, None),
        check_vma=False,
    )
```

```python
import functools

import jax
import jax.numpy as jnp
from jax import lax
from jax.experimental import pallas as pl
from jax.experimental.pallas import tpu as pltpu
from jax.sharding import Mesh
from jax.sharding import PartitionSpec as P


B = 512
SUB = 8
NB = 64
F32 = jnp.float32
BF = jnp.bfloat16
SIDES = (0, 1)
BASES = B // NB


def dot(a, b, ca, cb):
    return lax.dot_general(a, b, (((ca,), (cb,)), ((), ())), preferred_element_type=F32)


def cut(x):
    hi = x.astype(BF)
    return hi, (x - hi.astype(F32)).astype(BF)


def join(x):
    return x[0].astype(F32) + x[1].astype(F32)


def dot3(a, b, ca, cb):
    left = jnp.concatenate([a[0], a[0], a[1]], axis=ca)
    right = jnp.concatenate([b[0], b[1], b[0]], axis=cb)
    return dot(left, right, ca, cb)


def turn(x):
    return pltpu.roll(x, NB, 1)


def left_half(rows):
    return lax.broadcasted_iota(jnp.int32, (rows, 128), 1) < NB


def spread(x):
    left = left_half(x.shape[0])
    return jnp.concatenate([jnp.where(left, x, 0.0), jnp.where(left, 0.0, x)], axis=0)


def sb(x, i):
    return jnp.broadcast_to(x[i:i + 1, :], x.shape)


def lanes(x, idx):
    return jnp.take_along_axis(x, idx, axis=1, mode="promise_in_bounds")


def recip(p):
    r = pl.reciprocal(p, approx=True)
    return r, 2.0 - p * r


def invert_pair(D, fill):
    count = NB // SUB
    sub = lax.broadcasted_iota(jnp.int32, (SUB, 128), 0)
    lane = lax.broadcasted_iota(jnp.int32, (SUB, 128), 1)
    half = lane // NB * NB
    col = lane - half
    idx = [half + i for i in range(NB)]
    A = [D[SUB * r:SUB * (r + 1), :] for r in range(count)]
    W = [None] * count
    c = [lanes(A[0], idx[i]) for i in range(SUB)]
    for s in range(count):
        base = SUB * s
        more = s + 1 < count
        in_strip = (col >= base) & (col < base + SUB)
        unit = jnp.where(col == base + sub, 1.0, 0.0).astype(F32)
        ahead = [lanes(A[s], idx[base + SUB + j]) for j in range(SUB)] if more else []
        S = jnp.where(in_strip, unit, A[s])
        U = S
        scale = S
        for i in range(0, SUB, 2):
            at0, at1 = sub == i, sub == i + 1
            other = (sub < i) | (sub > i + 1)
            a, b, d = sb(c[i], i), sb(c[i], i + 1), sb(c[i + 1], i + 1)
            det = a * d - b * b
            rdet, fix = recip(det)
            rdet = rdet * fix
            m0 = jnp.where(other, -c[i], jnp.where(at0, 1.0, 0.0))
            m1 = jnp.where(other, -c[i + 1], jnp.where(at1, 1.0, 0.0))
            e0 = rdet * (m0 * d - m1 * b)
            e1 = rdet * (m1 * a - m0 * b)

            def eliminate(x):
                keep = jnp.where(other, x, 0.0)
                return keep + (e0 * sb(x, i) + e1 * sb(x, i + 1))

            ra, fix_a = recip(a)
            ra = ra * fix_a
            row0, row1 = sb(S, i), sb(S, i + 1)
            U = jnp.where(at0, row0, jnp.where(at1, row1 - (b * ra) * row0, U))
            scale = jnp.where(at0, lax.rsqrt(a), jnp.where(at1, lax.rsqrt(det * ra), scale))
            S = eliminate(S)
            for n in range(i + 2, SUB):
                c[n] = eliminate(c[n])
            ahead = [eliminate(x) for x in ahead]
        W[s] = jnp.where(col < base + SUB, U * scale, 0.0)
        z = [sb(S, i) for i in range(SUB)]
        for r in range(s + 1, count):
            X = A[r]
            x = [lanes(X, idx[base + i]) for i in range(SUB)]
            if r == s + 1:
                c = []
                for j in range(SUB):
                    t = [x[i] * sb(ahead[j], i) for i in range(SUB)]
                    c.append(lanes(X, idx[base + SUB + j]) - (((t[0] + t[1]) + (t[2] + t[3])) + ((t[4] + t[5]) + (t[6] + t[7]))))
            t = [x[i] * z[i] for i in range(SUB)]
            A[r] = jnp.where(in_strip, 0.0, X) - (((t[0] + t[1]) + (t[2] + t[3])) + ((t[4] + t[5]) + (t[6] + t[7])))
        fill()
    return jnp.concatenate(W, axis=0)


class Tasks:
    def __init__(self):
        self.open = []
        self.slots = BASES * (NB // SUB)
        self.base = 0

    def add(self, run, cost, last, needs=()):
        task = [run, cost, last, needs]
        self.open.append(task)
        return task

    def do(self, task):
        if task in self.open:
            self.open.remove(task)
            for other in task[3]:
                self.do(other)
            task[0]()

    def fill(self):
        self.slots -= 1
        left = self.slots % (NB // SUB) + 1
        urgent = sum(t[1] for t in self.open if t[2] <= self.base) / left
        even = sum(t[1] for t in self.open) / (self.slots + 1)
        share, done = max(urgent, even), 0.0
        while self.open and done < share:
            task = min(self.open, key=lambda t: t[2])
            done += task[1]
            self.do(task)

    def end_base(self):
        for task in [t for t in self.open if t[2] <= self.base]:
            self.do(task)
        self.base += 1

    def flush(self):
        while self.open:
            self.do(self.open[0])


def rows_of(i, n=128):
    return slice(n * i, n * (i + 1))


def kernel(g_ref, l0, ql0, r_hbm, qr_hbm, v_hbm, out_ref,
           r0, qr0, v0, lh, ll, ph, pl_, cp, kh, kl, uh, ul, q_scr, q_low, f_scr, n_scr, sem):
    copies = [pltpu.make_async_copy(source.at[0], target, sem.at[i])
              for i, (source, target) in enumerate(((r_hbm, r0), (qr_hbm, qr0), (v_hbm, v0)))]
    for copy in copies:
        copy.start()
    tasks = Tasks()
    old, basis = (l0, r0), (ql0, qr0)
    P = lambda m, r, c: (ph[m, r, c], pl_[m, r, c])
    every = slice(0, B)

    def project(m, r, c):
        ph[m, r, c], pl_[m, r, c] = cut(dot3((lh[m, r, :], ll[m, r, :]), cut(basis[m][:, c]), 1, 0))

    def correlate(r, c):
        both = [dot3(P(m, every, r), P(m, every, c), 0, 0) for m in SIDES]
        half = left_half(r.stop - r.start)
        for j in range((c.stop - c.start) // 128):
            l, x = (y[:, rows_of(j)] for y in both)
            at = 2 * c.start + 256 * j
            cp[r, at:at + 128] = jnp.where(half, l, turn(x))
            cp[r, at + 128:at + 256] = jnp.where(half, turn(l), x)

    lo, hi = slice(0, 256), slice(256, 512)
    for m in SIDES:
        g = g_ref[...]
        gram = 0.05 * dot(g, g, 1 - m, 1 - m)
        if m:
            copies[0].wait()
        lh[m], ll[m] = cut(0.95 * old[m][...] + gram)
        if m:
            copies[1].wait()
        project(m, every, lo)
    correlate(rows_of(0), rows_of(0))
    c_low = [tasks.add(lambda: correlate(rows_of(1), lo), 900, 0)]
    p_high = [tasks.add(lambda m=m: project(m, every, hi), 880, 1) for m in SIDES]
    c_low.append(tasks.add(lambda: correlate(hi, lo), 1200, 1, p_high))
    c_high = [tasks.add(lambda: correlate(hi, hi), 1200, 1, p_high)]

    def column(b):
        return slice(128 * b, 128 * (b + 1))

    K = lambda b, r: (kh[r, column(b)], kl[r, column(b)])
    w = [None] * BASES
    wd = [None] * BASES
    product = [None] * BASES
    w128 = [None] * 4
    k_rest = [None] * BASES
    move = [None] * 4

    def below(b, r):
        kh[r, column(b)], kl[r, column(b)] = cut(dot3(cut(cp[r, column(b)]), wd[b], 1, 1))

    def update(b, first, end, r):
        pairs = [cut(spread(join(K(b, rows_of(j, NB))))) for j in range(first, end)]
        right = [jnp.concatenate([x[i] for x in pairs], axis=0) for i in (0, 1)]
        c = slice(128 * first, 128 * end)
        cp[r, c] = cp[r, c] - dot3(K(b, r), right, 1, 1)

    def assemble(k):
        b = 2 * k
        half = left_half(NB)
        w1, w2 = w[b], w[b + 1]
        w21 = -dot3(cut(w2), cut(spread(product[b])), 1, 0)
        w128[k] = [cut(jnp.concatenate([jnp.where(half, w1, 0.0), jnp.where(half, w21, turn(w2))], axis=0)),
                   cut(jnp.concatenate([jnp.where(half, turn(w1), 0.0), jnp.where(half, turn(w21), w2)], axis=0))]

    def separate(k):
        r = slice(128 * (k + 1), B)
        half = left_half(B - r.start)
        a, c = join(K(2 * k, r)), join(K(2 * k + 1, r))
        uh[0, r, rows_of(k)], ul[0, r, rows_of(k)] = cut(jnp.where(half, a, turn(c)))
        uh[1, r, rows_of(k)], ul[1, r, rows_of(k)] = cut(jnp.where(half, turn(a), c))

    def solve(k, m):
        y = P(m, every, rows_of(k))
        if k:
            c = slice(0, 128 * k)
            done = (q_scr[m, :, c], q_low[m, :, c])
            y = cut(join(y) - dot3(done, (uh[m, rows_of(k), c], ul[m, rows_of(k), c]), 1, 1))
        q = dot3(y, w128[k][m], 1, 1)
        q_scr[m, :, rows_of(k)], q_low[m, :, rows_of(k)] = cut(q)

    def rotate(k):
        f_scr[rows_of(k), :] = dot(q_scr[0, :, rows_of(k)], g_ref[...], 0, 0).astype(BF)

    solved = []
    d = cp[0:NB, 0:128]
    for b in range(BASES):
        w[b] = invert_pair(d, tasks.fill)
        tasks.end_base()
        wd[b] = cut(spread(w[b]))
        if b + 1 < BASES:
            r = rows_of(b + 1, NB)
            below(b, r)
            x = join(K(b, r))
            d = cp[r, column(b + 1)] - dot3(cut(x), cut(spread(x)), 1, 1)
        if b % 2 == 0:
            def multiply(b=b):
                product[b] = dot3(K(b, rows_of(b + 1, NB)), wd[b], 1, 0)
            tasks.add(multiply, 100, b + 1)
        if b + 2 < BASES:
            rest = slice(NB * (b + 2), B)
            k_rest[b] = tasks.add(lambda b=b, rest=rest: below(b, rest), (B - rest.start) * 0.6, b + 1, c_low)
            tasks.add(lambda b=b, rest=rest: update(b, b + 1, b + 3, rest), 300 + B - rest.start, b + 1, [k_rest[b]])
            if b + 3 < BASES:
                far = slice(NB * (b + 3), B)
                tasks.add(lambda b=b, far=far: update(b, b + 3, BASES, far), 300 + (B - far.start) * (BASES - b - 3) * 0.5, b + 2,
                          [k_rest[b]] + (c_high if b < 2 else []))
        if b % 2:
            k = b // 2
            assembled = tasks.add(lambda k=k: assemble(k), 150, b + 2)
            needs = [assembled]
            if k < 3:
                needs.append(tasks.add(lambda k=k: separate(k), 200, b + 2, [k_rest[b - 1], k_rest[b]] if k_rest[b] else [k_rest[b - 1]]))
            solved = [tasks.add(lambda k=k, m=m: solve(k, m), 300 + 300 * k, b + 2, needs + solved + p_high)
                      for m in SIDES]
            tasks.add(lambda k=k: rotate(k), 300, b + 2, solved)
    tasks.flush()
    copies[2].wait()
    h = dot(f_scr[...], q_scr[1], 1, 0)
    v = 0.95 * v0[...] + 0.05 * h * h
    n_scr[...] = (h / (jnp.sqrt(v) + 1e-8)).astype(BF)
    e = dot(q_scr[0], n_scr[...], 1, 0).astype(BF)
    u = dot(e, q_scr[1], 1, 1)
    blocks = out_ref.shape[0]
    rows = B // blocks
    for c in range(4):
        out_ref[:, rows * c:rows * (c + 1), :] = u[:, 128 * c:128 * (c + 1)].astype(BF).reshape(blocks, rows, 128)
    total = jnp.broadcast_to(jnp.sum(u * u), (8, 128))
    first = total.astype(BF).astype(F32)
    second = (total - first).astype(BF).astype(F32)
    third = total - first - second
    row = lax.broadcasted_iota(jnp.int32, (8, 128), 0)
    tail = jnp.where(row == 0, first, jnp.where(row == 1, second, jnp.where(row == 2, third, 0.0)))
    out_ref[:, 4 * rows:, :] = jnp.broadcast_to(tail.astype(BF)[None], (blocks, 8, 128))


def stay(x):
    return pltpu.with_memory_space_constraint(x, pltpu.HBM)


def block_update(g, l0, r0, ql0, qr0, v0):
    vm = pl.BlockSpec(memory_space=pltpu.VMEM)
    hbm = pl.BlockSpec(memory_space=pl.ANY)
    return pl.pallas_call(
        kernel,
        out_shape=jax.ShapeDtypeStruct((16, B // 4 + 8, 128), BF),
        in_specs=[vm] * 3 + [hbm] * 3,
        out_specs=vm,
        name="update",
        scratch_shapes=[pltpu.VMEM((B, B), F32)] * 3
        + [pltpu.VMEM((2, B, B), BF)] * 4
        + [pltpu.VMEM((B, 2 * B), F32), pltpu.VMEM((B, 2 * B), BF), pltpu.VMEM((B, 2 * B), BF)]
        + [pltpu.VMEM((2, B, B), BF)] * 4
        + [pltpu.VMEM((B, B), BF)] * 2
        + [pltpu.SemaphoreType.DMA((3,))],
        compiler_params=pltpu.CompilerParams(vmem_limit_bytes=32 * 2**20),
    )(g, l0[0], ql0[0], stay(r0), stay(qr0), stay(v0))

FSDP = ("fsdp_0", "fsdp_1")
GROUP = ("group_0", "group_1")
FSDP_GROUP = ("fsdp_0", "fsdp_1", "group_0", "group_1")


def finish_kernel(owner_ref, total_ref, pieces_ref, out_ref, *, count):
    total = jnp.sum(total_ref[...], axis=0, keepdims=True)
    scale = jnp.minimum(1.0, 0.25 * jnp.sqrt(jnp.float32(count)) / jnp.sqrt(total + 1e-06))
    blocks, rows = out_ref.shape[0], out_ref.shape[1]
    scale = jnp.broadcast_to(scale, (rows, 128))
    first = pl.program_id(0) * blocks
    for j in range(blocks):
        owner = owner_ref[first + j]
        for c in range(B // 128):
            x = pieces_ref[owner, rows * c:rows * (c + 1), :].astype(jnp.float32)
            out_ref[j, :, 128 * c:128 * (c + 1)] = (scale * x).astype(jnp.bfloat16)


def finish(owner_row, totals, pieces, count):
    vm = pl.BlockSpec(memory_space=pltpu.VMEM)
    blocks = pieces.shape[0]
    steps = 4
    return pl.pallas_call(
        functools.partial(finish_kernel, count=count),
        out_shape=jax.ShapeDtypeStruct((blocks, B // blocks, B), jnp.bfloat16),
        grid=(steps,),
        in_specs=[pl.BlockSpec(memory_space=pltpu.SMEM), vm, vm],
        out_specs=pl.BlockSpec((blocks // steps, B // blocks, B), lambda i: (i, 0, 0)),
        name="finish",
        compiler_params=pltpu.CompilerParams(vmem_limit_bytes=4 * 2**20),
    )(owner_row, totals, pieces)


def on_device(gradients, owners, left_factors, right_factors, left_bases, right_bases, moments):
    fsdp_count, group_count = lax.axis_size(FSDP), lax.axis_size(GROUP)
    owner_row = owners[0]
    positions = jnp.arange(fsdp_count, dtype=jnp.int32)
    matches = owner_row[:, None] == positions[None, :]
    inverse = jnp.sum(jnp.where(matches, positions[:, None], 0), axis=0)
    outgoing = jnp.take(gradients, inverse, axis=0, mode="clip")
    gathered = lax.all_to_all(outgoing, FSDP, split_axis=0, concat_axis=0, tiled=True)
    packed = block_update(
        gathered.reshape(B, B), left_factors, right_factors, left_bases, right_bases, moments
    )
    pieces = lax.all_to_all(packed, FSDP, split_axis=0, concat_axis=0, tiled=True)
    squares = jnp.sum(pieces[:, B // 4:B // 4 + 3, :].astype(jnp.float32), axis=(0, 1))
    totals = lax.all_to_all(
        jnp.broadcast_to(squares[None], (group_count, 128)), GROUP, split_axis=0, concat_axis=0, tiled=True
    )
    return finish(owner_row, totals, pieces, fsdp_count * group_count * B * B)


def solution(mesh):
    split = Mesh(mesh.devices.reshape(4, 4, 4, 2), FSDP_GROUP)
    state = P(FSDP_GROUP, None, None)
    return jax.shard_map(
        on_device,
        mesh=split,
        in_specs=(P(GROUP, FSDP, None), P(GROUP, None), state, state, state, state, state),
        out_specs=P(GROUP, FSDP, None),
        check_vma=False,
    )
```

```python
import functools

import jax
import jax.numpy as jnp
from jax import lax
from jax.experimental import pallas as pl
from jax.experimental.pallas import tpu as pltpu
from jax.sharding import Mesh
from jax.sharding import PartitionSpec as P


B = 512
SUB = 8
NB = 64
F32 = jnp.float32
BF = jnp.bfloat16
SIDES = (0, 1)
BASES = B // NB


def dot(a, b, ca, cb):
    return lax.dot_general(a, b, (((ca,), (cb,)), ((), ())), preferred_element_type=F32)


def cut(x):
    hi = x.astype(BF)
    return hi, (x - hi.astype(F32)).astype(BF)


def join(x):
    return x[0].astype(F32) + x[1].astype(F32)


def dot3(a, b, ca, cb):
    left = jnp.concatenate([a[0], a[0], a[1]], axis=ca)
    right = jnp.concatenate([b[0], b[1], b[0]], axis=cb)
    return dot(left, right, ca, cb)


def turn(x):
    return pltpu.roll(x, NB, 1)


def left_half(rows):
    return lax.broadcasted_iota(jnp.int32, (rows, 128), 1) < NB


def spread(x):
    left = left_half(x.shape[0])
    return jnp.concatenate([jnp.where(left, x, 0.0), jnp.where(left, 0.0, x)], axis=0)


def sb(x, i):
    return jnp.broadcast_to(x[i:i + 1, :], x.shape)


def lanes(x, idx):
    return jnp.take_along_axis(x, idx, axis=1, mode="promise_in_bounds")


def recip(p):
    r = pl.reciprocal(p, approx=True)
    return r, 2.0 - p * r


def invert_pair(D, fill):
    count = NB // SUB
    sub = lax.broadcasted_iota(jnp.int32, (SUB, 128), 0)
    lane = lax.broadcasted_iota(jnp.int32, (SUB, 128), 1)
    half = lane // NB * NB
    col = lane - half
    idx = [half + i for i in range(NB)]
    A = [D[SUB * r:SUB * (r + 1), :] for r in range(count)]
    W = [None] * count
    c = [lanes(A[0], idx[i]) for i in range(SUB)]
    for s in range(count):
        base = SUB * s
        more = s + 1 < count
        in_strip = (col >= base) & (col < base + SUB)
        unit = jnp.where(col == base + sub, 1.0, 0.0).astype(F32)
        ahead = [lanes(A[s], idx[base + SUB + j]) for j in range(SUB)] if more else []
        S = jnp.where(in_strip, unit, A[s])
        U = S
        scale = S
        for i in range(0, SUB, 2):
            at0, at1 = sub == i, sub == i + 1
            other = (sub < i) | (sub > i + 1)
            a, b, d = sb(c[i], i), sb(c[i], i + 1), sb(c[i + 1], i + 1)
            det = a * d - b * b
            rdet, fix = recip(det)
            rdet = rdet * fix
            m0 = jnp.where(other, -c[i], jnp.where(at0, 1.0, 0.0))
            m1 = jnp.where(other, -c[i + 1], jnp.where(at1, 1.0, 0.0))
            e0 = rdet * (m0 * d - m1 * b)
            e1 = rdet * (m1 * a - m0 * b)

            def eliminate(x):
                keep = jnp.where(other, x, 0.0)
                return keep + (e0 * sb(x, i) + e1 * sb(x, i + 1))

            ra, fix_a = recip(a)
            ra = ra * fix_a
            row0, row1 = sb(S, i), sb(S, i + 1)
            U = jnp.where(at0, row0, jnp.where(at1, row1 - (b * ra) * row0, U))
            scale = jnp.where(at0, lax.rsqrt(a), jnp.where(at1, lax.rsqrt(det * ra), scale))
            S = eliminate(S)
            for n in range(i + 2, SUB):
                c[n] = eliminate(c[n])
            ahead = [eliminate(x) for x in ahead]
        W[s] = jnp.where(col < base + SUB, U * scale, 0.0)
        z = [sb(S, i) for i in range(SUB)]
        for r in range(s + 1, count):
            X = A[r]
            x = [lanes(X, idx[base + i]) for i in range(SUB)]
            if r == s + 1:
                c = []
                for j in range(SUB):
                    t = [x[i] * sb(ahead[j], i) for i in range(SUB)]
                    c.append(lanes(X, idx[base + SUB + j]) - (((t[0] + t[1]) + (t[2] + t[3])) + ((t[4] + t[5]) + (t[6] + t[7]))))
            t = [x[i] * z[i] for i in range(SUB)]
            A[r] = jnp.where(in_strip, 0.0, X) - (((t[0] + t[1]) + (t[2] + t[3])) + ((t[4] + t[5]) + (t[6] + t[7])))
        fill()
    return jnp.concatenate(W, axis=0)


class Tasks:
    def __init__(self):
        self.open = []
        self.slots = BASES * (NB // SUB)
        self.base = 0

    def add(self, run, cost, last, needs=()):
        task = [run, cost, last, needs]
        self.open.append(task)
        return task

    def do(self, task):
        if task in self.open:
            self.open.remove(task)
            for other in task[3]:
                self.do(other)
            task[0]()

    def fill(self):
        self.slots -= 1
        left = self.slots % (NB // SUB) + 1
        urgent = sum(t[1] for t in self.open if t[2] <= self.base) / left
        even = sum(t[1] for t in self.open) / (self.slots + 1)
        share, done = max(urgent, even), 0.0
        while self.open and done < share:
            task = min(self.open, key=lambda t: t[2])
            done += task[1]
            self.do(task)

    def end_base(self):
        for task in [t for t in self.open if t[2] <= self.base]:
            self.do(task)
        self.base += 1

    def flush(self):
        while self.open:
            self.do(self.open[0])


def rows_of(i, n=128):
    return slice(n * i, n * (i + 1))


def kernel(g_ref, l0, ql0, r_hbm, qr_hbm, v_hbm, out_ref,
           r0, qr0, v0, lh, ll, ph, pl_, cp, kh, kl, uh, ul, q_scr, q_low, f_scr, n_scr, sem):
    copies = [pltpu.make_async_copy(source.at[0], target, sem.at[i])
              for i, (source, target) in enumerate(((r_hbm, r0), (qr_hbm, qr0), (v_hbm, v0)))]
    for copy in copies:
        copy.start()
    tasks = Tasks()
    old, basis = (l0, r0), (ql0, qr0)
    P = lambda m, r, c: (ph[m, r, c], pl_[m, r, c])
    every = slice(0, B)

    def project(m, r, c):
        ph[m, r, c], pl_[m, r, c] = cut(dot3((lh[m, r, :], ll[m, r, :]), cut(basis[m][:, c]), 1, 0))

    def correlate(r, c):
        both = [dot3(P(m, every, r), P(m, every, c), 0, 0) for m in SIDES]
        half = left_half(r.stop - r.start)
        for j in range((c.stop - c.start) // 128):
            l, x = (y[:, rows_of(j)] for y in both)
            at = 2 * c.start + 256 * j
            cp[r, at:at + 128] = jnp.where(half, l, turn(x))
            cp[r, at + 128:at + 256] = jnp.where(half, turn(l), x)

    lo, hi = slice(0, 256), slice(256, 512)
    for m in SIDES:
        g = g_ref[...]
        gram = 0.05 * dot(g, g, 1 - m, 1 - m)
        if m:
            copies[0].wait()
        lh[m], ll[m] = cut(0.95 * old[m][...] + gram)
        if m:
            copies[1].wait()
        project(m, every, lo)
    correlate(rows_of(0), rows_of(0))
    c_low = [tasks.add(lambda: correlate(rows_of(1), lo), 900, 0)]
    p_high = [tasks.add(lambda m=m: project(m, every, hi), 880, 1) for m in SIDES]
    c_low.append(tasks.add(lambda: correlate(hi, lo), 1200, 1, p_high))
    c_high = [tasks.add(lambda: correlate(hi, hi), 1200, 1, p_high)]

    def column(b):
        return slice(128 * b, 128 * (b + 1))

    K = lambda b, r: (kh[r, column(b)], kl[r, column(b)])
    w = [None] * BASES
    wd = [None] * BASES
    product = [None] * BASES
    w128 = [None] * 4
    k_rest = [None] * BASES
    move = [None] * 4

    def below(b, r):
        kh[r, column(b)], kl[r, column(b)] = cut(dot3(cut(cp[r, column(b)]), wd[b], 1, 1))

    def update(b, first, end, r):
        pairs = [cut(spread(join(K(b, rows_of(j, NB))))) for j in range(first, end)]
        right = [jnp.concatenate([x[i] for x in pairs], axis=0) for i in (0, 1)]
        c = slice(128 * first, 128 * end)
        cp[r, c] = cp[r, c] - dot3(K(b, r), right, 1, 1)

    def assemble(k):
        b = 2 * k
        half = left_half(NB)
        w1, w2 = w[b], w[b + 1]
        w21 = -dot3(cut(w2), cut(spread(product[b])), 1, 0)
        w128[k] = [cut(jnp.concatenate([jnp.where(half, w1, 0.0), jnp.where(half, w21, turn(w2))], axis=0)),
                   cut(jnp.concatenate([jnp.where(half, turn(w1), 0.0), jnp.where(half, turn(w21), w2)], axis=0))]

    def separate(k):
        r = slice(128 * (k + 1), B)
        half = left_half(B - r.start)
        a, c = join(K(2 * k, r)), join(K(2 * k + 1, r))
        uh[0, r, rows_of(k)], ul[0, r, rows_of(k)] = cut(jnp.where(half, a, turn(c)))
        uh[1, r, rows_of(k)], ul[1, r, rows_of(k)] = cut(jnp.where(half, turn(a), c))

    def prepare(k, m):
        c = slice(0, 128 * k)
        done = (q_scr[m, :, c], q_low[m, :, c])
        y = join(P(m, every, rows_of(k))) - dot3(done, (uh[m, rows_of(k), c], ul[m, rows_of(k), c]), 1, 1)
        ph[m, :, rows_of(k)], pl_[m, :, rows_of(k)] = cut(y)

    def solve(k, m):
        q = dot3(P(m, every, rows_of(k)), w128[k][m], 1, 1)
        q_scr[m, :, rows_of(k)], q_low[m, :, rows_of(k)] = cut(q)

    def rotate(k):
        f_scr[rows_of(k), :] = dot(q_scr[0, :, rows_of(k)], g_ref[...], 0, 0).astype(BF)

    ready = []
    d = cp[0:NB, 0:128]
    for b in range(BASES):
        w[b] = invert_pair(d, tasks.fill)
        tasks.end_base()
        wd[b] = cut(spread(w[b]))
        if b + 1 < BASES:
            r = rows_of(b + 1, NB)
            below(b, r)
            x = join(K(b, r))
            d = cp[r, column(b + 1)] - dot3(cut(x), cut(spread(x)), 1, 1)
        if b % 2 == 0:
            def multiply(b=b):
                product[b] = dot3(K(b, rows_of(b + 1, NB)), wd[b], 1, 0)
            tasks.add(multiply, 100, b + 1)
        if b + 2 < BASES:
            rest = slice(NB * (b + 2), B)
            k_rest[b] = tasks.add(lambda b=b, rest=rest: below(b, rest), (B - rest.start) * 0.6, b + 1, c_low)
            tasks.add(lambda b=b, rest=rest: update(b, b + 1, b + 3, rest), 300 + B - rest.start, b + 1, [k_rest[b]])
            if b + 3 < BASES:
                far = slice(NB * (b + 3), B)
                tasks.add(lambda b=b, far=far: update(b, b + 3, BASES, far), 300 + (B - far.start) * (BASES - b - 3) * 0.5, b + 2,
                          [k_rest[b]] + (c_high if b < 2 else []))
        if b % 2:
            k = b // 2
            assembled = tasks.add(lambda k=k: assemble(k), 150, b + 2)
            needs = [assembled]
            if k < 3:
                needs.append(tasks.add(lambda k=k: separate(k), 200, b + 2, [k_rest[b - 1], k_rest[b]] if k_rest[b] else [k_rest[b - 1]]))
            solved = [tasks.add(lambda k=k, m=m: solve(k, m), 300, b + 2, needs + ready + p_high)
                      for m in SIDES]
            tasks.add(lambda k=k: rotate(k), 300, b + 2, solved)
            if k < 3:
                ready = [tasks.add(lambda k=k, m=m: prepare(k + 1, m), 300 * (k + 1), b + 2, solved + needs) for m in SIDES]
    tasks.flush()
    copies[2].wait()
    h = dot(f_scr[...], q_scr[1], 1, 0)
    v = 0.95 * v0[...] + 0.05 * h * h
    n_scr[...] = (h / (jnp.sqrt(v) + 1e-8)).astype(BF)
    e = dot(q_scr[0], n_scr[...], 1, 0).astype(BF)
    u = dot(e, q_scr[1], 1, 1)
    blocks = out_ref.shape[0]
    rows = B // blocks
    for c in range(4):
        out_ref[:, rows * c:rows * (c + 1), :] = u[:, 128 * c:128 * (c + 1)].astype(BF).reshape(blocks, rows, 128)
    total = jnp.broadcast_to(jnp.sum(u * u), (8, 128))
    first = total.astype(BF).astype(F32)
    second = (total - first).astype(BF).astype(F32)
    third = total - first - second
    row = lax.broadcasted_iota(jnp.int32, (8, 128), 0)
    tail = jnp.where(row == 0, first, jnp.where(row == 1, second, jnp.where(row == 2, third, 0.0)))
    out_ref[:, 4 * rows:, :] = jnp.broadcast_to(tail.astype(BF)[None], (blocks, 8, 128))


def stay(x):
    return pltpu.with_memory_space_constraint(x, pltpu.HBM)


def block_update(g, l0, r0, ql0, qr0, v0):
    vm = pl.BlockSpec(memory_space=pltpu.VMEM)
    hbm = pl.BlockSpec(memory_space=pl.ANY)
    return pl.pallas_call(
        kernel,
        out_shape=jax.ShapeDtypeStruct((16, B // 4 + 8, 128), BF),
        in_specs=[vm] * 3 + [hbm] * 3,
        out_specs=vm,
        name="update",
        scratch_shapes=[pltpu.VMEM((B, B), F32)] * 3
        + [pltpu.VMEM((2, B, B), BF)] * 4
        + [pltpu.VMEM((B, 2 * B), F32), pltpu.VMEM((B, 2 * B), BF), pltpu.VMEM((B, 2 * B), BF)]
        + [pltpu.VMEM((2, B, B), BF)] * 4
        + [pltpu.VMEM((B, B), BF)] * 2
        + [pltpu.SemaphoreType.DMA((3,))],
        compiler_params=pltpu.CompilerParams(vmem_limit_bytes=32 * 2**20),
    )(g, l0[0], ql0[0], stay(r0), stay(qr0), stay(v0))

FSDP = ("fsdp_0", "fsdp_1")
GROUP = ("group_0", "group_1")
FSDP_GROUP = ("fsdp_0", "fsdp_1", "group_0", "group_1")


def finish_kernel(owner_ref, total_ref, pieces_ref, out_ref, *, count):
    total = jnp.sum(total_ref[...], axis=0, keepdims=True)
    scale = jnp.minimum(1.0, 0.25 * jnp.sqrt(jnp.float32(count)) / jnp.sqrt(total + 1e-06))
    blocks, rows = out_ref.shape[0], out_ref.shape[1]
    scale = jnp.broadcast_to(scale, (rows, 128))
    first = pl.program_id(0) * blocks
    for j in range(blocks):
        owner = owner_ref[first + j]
        for c in range(B // 128):
            x = pieces_ref[owner, rows * c:rows * (c + 1), :].astype(jnp.float32)
            out_ref[j, :, 128 * c:128 * (c + 1)] = (scale * x).astype(jnp.bfloat16)


def finish(owner_row, totals, pieces, count):
    vm = pl.BlockSpec(memory_space=pltpu.VMEM)
    blocks = pieces.shape[0]
    steps = 4
    return pl.pallas_call(
        functools.partial(finish_kernel, count=count),
        out_shape=jax.ShapeDtypeStruct((blocks, B // blocks, B), jnp.bfloat16),
        grid=(steps,),
        in_specs=[pl.BlockSpec(memory_space=pltpu.SMEM), vm, vm],
        out_specs=pl.BlockSpec((blocks // steps, B // blocks, B), lambda i: (i, 0, 0)),
        name="finish",
        compiler_params=pltpu.CompilerParams(vmem_limit_bytes=4 * 2**20),
    )(owner_row, totals, pieces)


def on_device(gradients, owners, left_factors, right_factors, left_bases, right_bases, moments):
    fsdp_count, group_count = lax.axis_size(FSDP), lax.axis_size(GROUP)
    owner_row = owners[0]
    positions = jnp.arange(fsdp_count, dtype=jnp.int32)
    matches = owner_row[:, None] == positions[None, :]
    inverse = jnp.sum(jnp.where(matches, positions[:, None], 0), axis=0)
    outgoing = jnp.take(gradients, inverse, axis=0, mode="clip")
    gathered = lax.all_to_all(outgoing, FSDP, split_axis=0, concat_axis=0, tiled=True)
    packed = block_update(
        gathered.reshape(B, B), left_factors, right_factors, left_bases, right_bases, moments
    )
    pieces = lax.all_to_all(packed, FSDP, split_axis=0, concat_axis=0, tiled=True)
    squares = jnp.sum(pieces[:, B // 4:B // 4 + 3, :].astype(jnp.float32), axis=(0, 1))
    totals = lax.all_to_all(
        jnp.broadcast_to(squares[None], (group_count, 128)), GROUP, split_axis=0, concat_axis=0, tiled=True
    )
    return finish(owner_row, totals, pieces, fsdp_count * group_count * B * B)


def solution(mesh):
    split = Mesh(mesh.devices.reshape(4, 4, 4, 2), FSDP_GROUP)
    state = P(FSDP_GROUP, None, None)
    return jax.shard_map(
        on_device,
        mesh=split,
        in_specs=(P(GROUP, FSDP, None), P(GROUP, None), state, state, state, state, state),
        out_specs=P(GROUP, FSDP, None),
        check_vma=False,
    )
```
